512 devices in a mesh: tube: 32 (over z, y_lo), gy: 4 (over y_hi, core), gz: 4 (over x).
Axes of the slice: x: 4, y: 4 (y_hi: 2, y_lo: 2; y = y_hi * 2 + y_lo), z: 16, core: 2. Of those that a mesh axis runs over, the one named last changes fastest.
Arguments:
- state: float32 [13, 512, 32, 512], P(None, 'tube', 'gy', 'gz'), as said below
- fresh: float32 [13, 32, 512], P(None, 'gy', 'gz'), as said below
- substeps: int32 [512, 32, 512], P('tube', 'gy', 'gz'), may hold values from 1 to 8, as said below
- shift: int32 [], replicated, may hold values from 1 to 12
Outputs:
- advanced: float32 [13, 512, 32, 512], P(None, 'tube', 'gy', 'gz')
The draws below stay inside these ranges and needn't reach their ends.
Inputs may be any that keep to these rules, and one draw needn't show every extreme that they name: `state`: the first nine components are positive partial densities; the energy exceeds the kinetic and chemical energy by a positive thermal part. `fresh`: the same conventions as state. `substeps`: at most 8; some cell takes 8 in every draw.
All inputs are finite; a program needn't handle non-finite values.
Results may differ from the reference program's by a relative error of at most 0.0003.
Values sent between devices are 32-bit elements; how exact they have to be, the bound alone decides.
A program may use at most 64 MiB of HBM per device.

```python
import jax
import jax.numpy as jnp
import numpy as np
from jax import lax

SMAX = 12
CMAX = 8
NX = 512
NY = 32
NZ = 512


molar_table = [2.016 / 18.015, 31.998 / 18.015, 18.015 / 18.015, 1.008 / 18.015, 15.999 / 18.015, 17.007 / 18.015, 33.006 / 18.015, 34.014 / 18.015, 28.014 / 18.015]


factor_table = [2.5, 2.5, 3.0, 1.5, 1.5, 2.5, 3.0, 3.0, 2.5]


energy_table = [0.0, 0.0, -1.5, 12.0, 1.5, 0.25, 0.02, -0.45, 0.0]


burnt_base = [0.03, 0.15, 0.3, 0.01, 0.02, 0.04, 0.005, 0.005, 0.7]


fresh_base = [0.06, 0.25, 0.02, 0.004, 0.004, 0.006, 0.002, 0.002, 0.75]


def gas_sample(key, grid_extents, base):
    stochastic_seeds = jax.random.split(key, 4)
    lead = (1,) * len(grid_extents)
    base_col = jnp.asarray(base, jnp.float32).reshape((9,) + lead)
    constituent_grids = base_col * jnp.exp(jax.random.uniform(stochastic_seeds[0], (9,) + grid_extents, jnp.float32, -0.7, 0.7))
    stir = 0.25 * jnp.clip(jax.random.normal(stochastic_seeds[1], (3,) + grid_extents, jnp.float32), -3.0, 3.0)
    kelvin_level = jax.random.uniform(stochastic_seeds[2], grid_extents, jnp.float32, 1.0, 2.2)
    drift = jnp.asarray([-1.0, 0.0, 0.0], jnp.float32).reshape((3,) + lead)
    if len(grid_extents) == 3:
        plane_seeds = jax.random.split(stochastic_seeds[3], 3)
        plane_shape = (grid_extents[0], 1, 1)
        plane_density = jnp.exp(jax.random.uniform(plane_seeds[0], plane_shape, jnp.float32, -1.0, 1.0))
        plane_heat = jax.random.uniform(plane_seeds[1], plane_shape, jnp.float32, 0.75, 1.35)
        plane_speed = jax.random.uniform(plane_seeds[2], plane_shape, jnp.float32, -0.5, 0.5)
        constituent_grids = constituent_grids * plane_density[None]
        kelvin_level = kelvin_level * plane_heat
        drift = drift + jnp.concatenate([plane_speed[None], jnp.zeros((2,) + plane_shape, jnp.float32)], axis=0)
    fluid_speed_vector = drift + stir
    kilograms_per_volume = jnp.sum(constituent_grids, axis=0)
    calorific_entries = jnp.asarray([factor_table[constituent_count] / molar_table[constituent_count] for constituent_count in range(9)], jnp.float32).reshape((9,) + lead)
    enthalpy_of_creation = jnp.asarray(energy_table, jnp.float32).reshape((9,) + lead)
    overall_conserved_work = jnp.sum(constituent_grids * calorific_entries, axis=0) * kelvin_level + jnp.sum(constituent_grids * enthalpy_of_creation, axis=0) + 0.5 * kilograms_per_volume * jnp.sum(fluid_speed_vector * fluid_speed_vector, axis=0)
    return jnp.concatenate([constituent_grids, kilograms_per_volume[None] * fluid_speed_vector, overall_conserved_work[None]], axis=0)


def draw_state(key, part):
    return gas_sample(jax.random.fold_in(key, 11), (NX, NY, NZ), burnt_base)


def draw_fresh(key, part):
    return gas_sample(jax.random.fold_in(key, 23), (NY, NZ), fresh_base)


def draw_substeps(key, part):
    plane = lax.broadcasted_iota(jnp.int32, (NX, NY, NZ), 0)
    band = plane >= NX - max(NX // 8, 1)
    top = jnp.where(band, CMAX, 2)
    raw = jax.random.randint(jax.random.fold_in(key, 37), (NX, NY, NZ), 0, 1 << 20)
    counts = 1 + raw % top
    return counts.at[NX - 1, NY - 1, NZ - 1].set(CMAX)


def setup_inputs(seed: int = 0) -> dict:
    keys = jax.random.split(jax.random.key(seed), 5)
    state = draw_state(jax.random.fold_in(keys[4], 71), 0)
    fresh = draw_fresh(jax.random.fold_in(keys[4], 71), 0)
    substeps = draw_substeps(jax.random.fold_in(keys[4], 71), 0)
    shift = jax.random.randint(keys[3], (), 1, SMAX + 1).astype(jnp.int32)
    return {"state": state, "fresh": fresh, "substeps": substeps, "shift": shift}


molar_mass = np.array([2.016, 31.998, 18.015, 1.008, 15.999, 17.007, 33.006, 34.014, 28.014]) / 18.015
heat_factor = np.array([2.5, 2.5, 3.0, 1.5, 1.5, 2.5, 3.0, 3.0, 2.5])
formation = np.array([0.0, 0.0, -1.5, 12.0, 1.5, 0.25, 0.02, -0.45, 0.0])
consumed_stoichiometry = [(3, 1, 9), (4, 5, 9), (4, 0, 9), (3, 5, 9), (0, 5, 9), (2, 3, 9), (4, 2, 9), (5, 5, 9), (0, 8, 9), (3, 3, 8), (4, 4, 8), (3, 4, 8), (3, 5, 8), (3, 1, 8), (6, 3, 9), (6, 3, 9), (6, 4, 9), (6, 5, 9), (6, 6, 9), (7, 8, 9), (7, 3, 9)]
products = [(4, 5), (3, 1), (3, 5), (4, 0), (2, 3), (0, 5), (5, 5), (4, 2), (3, 3), (0,), (1,), (5,), (2,), (6,), (0, 1), (5, 5), (1, 5), (2, 1), (7, 1), (5, 5), (2, 5)]
arrhenius_coefficients = [30.0, 8.0, 20.0, 6.0, 25.0, 10.0, 12.0, 5.0, 4.0, 20.0, 15.0, 18.0, 22.0, 25.0, 30.0, 25.0, 20.0, 30.0, 10.0, 6.0, 15.0]
arrhenius_barrier = [4.0, 1.0, 3.0, 1.5, 1.5, 4.5, 4.0, 1.5, 6.0, 0.5, 0.5, 0.5, 0.5, 0.3, 0.8, 0.5, 0.3, 0.3, 0.5, 5.0, 1.5]
time_step = 0.05

def stoich_table():
    table = np.zeros((9, 21))
    for constituent_count in range(21):
        for which in consumed_stoichiometry[constituent_count]:
            if which < 9:
                table[which, constituent_count] -= 1.0
        for which in products[constituent_count]:
            table[which, constituent_count] += 1.0
    return table * molar_mass[:, None]

def column(values, array):
    return jnp.asarray(values, dtype=array.dtype).reshape((9,) + (1,) * (array.ndim - 1))

def weno_side(first, second, third, fourth, fifth):
    smooth_a = 13.0 / 12.0 * (first - 2.0 * second + third) ** 2 + 0.25 * (first - 4.0 * second + 3.0 * third) ** 2
    smooth_b = 13.0 / 12.0 * (second - 2.0 * third + fourth) ** 2 + 0.25 * (second - fourth) ** 2
    smooth_c = 13.0 / 12.0 * (third - 2.0 * fourth + fifth) ** 2 + 0.25 * (3.0 * third - 4.0 * fourth + fifth) ** 2
    weight_a = 0.1 / (1e-06 + smooth_a) ** 2
    weight_b = 0.6 / (1e-06 + smooth_b) ** 2
    weight_c = 0.3 / (1e-06 + smooth_c) ** 2
    total = weight_a + weight_b + weight_c
    blend = weight_a * (2.0 * first - 7.0 * second + 11.0 * third) + weight_b * (-second + 5.0 * third + 2.0 * fourth) + weight_c * (2.0 * third + 5.0 * fourth - fifth)
    return blend / (6.0 * total)

def flux_change(ghosted_grid_values, array_axis, count):
    constituent_grids = ghosted_grid_values[:9]
    kilograms_per_volume = lax.optimization_barrier(jnp.sum(constituent_grids, axis=0))
    momentum = ghosted_grid_values[9:12]
    motion_work = 0.5 * lax.optimization_barrier(jnp.sum(momentum * momentum, axis=0)) / kilograms_per_volume
    specific_warming_coefficient = lax.optimization_barrier(jnp.sum(constituent_grids * column(heat_factor / molar_mass, constituent_grids), axis=0))
    combustion_portion = lax.optimization_barrier(jnp.sum(constituent_grids * column(formation, constituent_grids), axis=0))
    kelvin_level = (ghosted_grid_values[12] - motion_work - combustion_portion) / specific_warming_coefficient
    blend_accumulation = lax.optimization_barrier(jnp.sum(constituent_grids * column(1.0 / molar_mass, constituent_grids), axis=0))
    thermodynamic_stress = blend_accumulation * kelvin_level
    sound = jnp.sqrt((1.0 + blend_accumulation / specific_warming_coefficient) * thermodynamic_stress / kilograms_per_volume)
    row = 8 + array_axis
    fluid_speed_vector = ghosted_grid_values[row] / kilograms_per_volume
    flux = ghosted_grid_values * fluid_speed_vector[None]
    flux = jnp.concatenate([flux[:row], (flux[row] + thermodynamic_stress)[None], flux[row + 1:12], (flux[12] + thermodynamic_stress * fluid_speed_vector)[None]], axis=0)
    speed = (jnp.abs(fluid_speed_vector) + sound)[None]

    def take(array, offset):
        return lax.slice_in_dim(array, offset, offset + count + 1, axis=array_axis)
    alpha = take(speed, 0)
    for offset in range(1, 6):
        alpha = jnp.maximum(alpha, take(speed, offset))
    plus = [0.5 * (take(flux, offset) + alpha * take(ghosted_grid_values, offset)) for offset in range(5)]
    minus = [0.5 * (take(flux, offset) - alpha * take(ghosted_grid_values, offset)) for offset in range(1, 6)]
    face = weno_side(plus[0], plus[1], plus[2], plus[3], plus[4]) + weno_side(minus[4], minus[3], minus[2], minus[1], minus[0])
    return lax.slice_in_dim(face, 1, count + 1, axis=array_axis) - lax.slice_in_dim(face, 0, count, axis=array_axis)

def react_step(constituent_grids, thermal_content, step_size):
    specific_warming_coefficient = lax.optimization_barrier(jnp.sum(constituent_grids * column(heat_factor / molar_mass, constituent_grids), axis=0))
    combustion_portion = lax.optimization_barrier(jnp.sum(constituent_grids * column(formation, constituent_grids), axis=0))
    kelvin_level = (thermal_content - combustion_portion) / specific_warming_coefficient
    moles_per_volume = constituent_grids * column(1.0 / molar_mass, constituent_grids)
    moles_per_volume = jnp.concatenate([moles_per_volume, jnp.ones_like(moles_per_volume[:1])], axis=0)
    progress_speeds = jnp.stack([arrhenius_coefficients[constituent_count] * jnp.exp(-arrhenius_barrier[constituent_count] / kelvin_level) * moles_per_volume[consumed_stoichiometry[constituent_count][0]] * moles_per_volume[consumed_stoichiometry[constituent_count][1]] * moles_per_volume[consumed_stoichiometry[constituent_count][2]] for constituent_count in range(21)])
    table = jnp.asarray(stoich_table(), dtype=constituent_grids.dtype)
    omega = jnp.dot(table, progress_speeds, precision=lax.Precision.HIGHEST)
    return constituent_grids + step_size[None] * omega

def react_cells(constituent_grids, thermal_content, counts, turns):
    step_size = time_step / counts.astype(constituent_grids.dtype)

    def advance(index, current):
        moved = react_step(current, thermal_content, step_size)
        return jnp.where((index < counts)[None], moved, current)
    return lax.fori_loop(0, turns, advance, constituent_grids)

def reference(state, fresh, substeps, shift):
    comps, planes, width_y, width_z = state.shape
    inflow = jnp.broadcast_to(fresh[:, None], (comps, SMAX, width_y, width_z))
    joined = jnp.concatenate([state, inflow], axis=1)
    start = lax.dynamic_slice_in_dim(joined, shift.astype(jnp.int32), planes, 1)
    ghosts = jnp.broadcast_to(fresh[:, None], (comps, 3, width_y, width_z))

    def evaluate(current):
        edge = jnp.broadcast_to(current[:, :1], (comps, 3, width_y, width_z))
        x_ext = jnp.concatenate([edge, current, ghosts], axis=1)
        y_ext = jnp.pad(current, ((0, 0), (0, 0), (3, 3), (0, 0)), mode='wrap')
        z_ext = jnp.pad(current, ((0, 0), (0, 0), (0, 0), (3, 3)), mode='wrap')

        def strip(index):
            lower = index * 4
            x_part = lax.dynamic_slice_in_dim(x_ext, lower, 4, 2)
            y_part = lax.dynamic_slice_in_dim(y_ext, lower, 10, 2)
            z_part = lax.dynamic_slice_in_dim(z_ext, lower, 4, 2)
            return -(flux_change(x_part, 1, planes) + flux_change(y_part, 2, 4) + flux_change(z_part, 3, width_z))
        stacked = lax.map(strip, jnp.arange(width_y // 4))
        return jnp.transpose(stacked, (1, 2, 0, 3, 4)).reshape(comps, planes, width_y, width_z)
    first = start + time_step * evaluate(start)
    second = 0.75 * start + 0.25 * (first + time_step * evaluate(first))
    third = 1.0 / 3.0 * start + 2.0 / 3.0 * (second + time_step * evaluate(second))
    kilograms_per_volume = lax.optimization_barrier(jnp.sum(third[:9], axis=0))
    thermal_content = third[12] - 0.5 * lax.optimization_barrier(jnp.sum(third[9:12] * third[9:12], axis=0)) / kilograms_per_volume
    cells = planes * width_y * width_z
    reacted = react_cells(third[:9].reshape(9, cells), thermal_content.reshape(cells), substeps.reshape(cells), CMAX)
    return jnp.concatenate([reacted.reshape(9, planes, width_y, width_z), third[9:]], axis=0)
```

```python
import functools

import jax
import jax.numpy as jnp
import numpy as np
from jax import lax
from jax.experimental import pallas as pl
from jax.experimental.pallas import tpu as pltpu
from jax.sharding import PartitionSpec as P

SMAX = 12
CMAX = 8
DT = 0.05
W = [float(w) for w in np.array([2.016, 31.998, 18.015, 1.008, 15.999, 17.007, 33.006, 34.014, 28.014]) / 18.015]
IW = [1.0 / w for w in W]
MESH = pl.DeviceIdType.MESH
F32 = jnp.float32


def total(parts):
    while len(parts) > 1:
        parts = [a + b for a, b in zip(parts[::2], parts[1::2])] + ([parts[-1]] if len(parts) % 2 else [])
    return parts[0]


def gas(u):
    rho = total(list(u[:9]))
    c = [u[k] * IW[k] for k in range(9)]
    s1 = total([c[0], c[1], c[5], c[8]])
    s2 = total([c[2], c[6], c[7]])
    s3 = c[3] + c[4]
    gas_sum = s1 + s2 + s3
    heat = 2.5 * s1 + 3.0 * s2 + 1.5 * s3
    bound = total([-1.5 * u[2], 12.0 * u[3], 1.5 * u[4], 0.25 * u[5], 0.02 * u[6], -0.45 * u[7]])
    r = 1.0 / rho
    kinetic = 0.5 * r * (u[9] * u[9] + u[10] * u[10] + u[11] * u[11])
    over = 1.0 / heat
    pressure = gas_sum * ((u[12] - kinetic - bound) * over)
    sound = jnp.sqrt((1.0 + gas_sum * over) * pressure * r)
    return r, pressure, sound


def one_side(e1, e2, e3, e4):
    k2 = e2 * e2 * 0.609375 + 3e-6
    k3 = e3 * e3 * 0.609375 + 3e-6
    ta = e1 - 1.375 * e2
    tb = e3 - 0.625 * e2
    tc = e4 - 1.375 * e3
    ra = 1.0 / (ta * ta + k2)
    rb = 1.0 / (tb * tb + k2)
    rc = 1.0 / (tc * tc + k3)
    d23 = e3 - e2
    a = ta + tb
    c = d23 - (e4 - e3)
    wa = ra * ra
    wb = rb * rb * 6.0
    wc = rc * rc * 3.0
    return (wc * c - wa * (a + a)) / (wa + wb + wc) - d23


def face(pair_sum, alpha, df, du):
    p = [alpha * d for d in du]
    plus = [df[k] + p[k] for k in range(4)]
    minus = [df[k] - p[k] for k in range(1, 5)]
    x = one_side(plus[0], plus[1], plus[2], plus[3])
    y = one_side(minus[3], minus[2], minus[1], minus[0])
    return 6.0 * pair_sum + (x - y)


def sweep(lo, hi, value, speed, extra, kind, alpha, emit, before=None, after=None):
    us, fs, du, df = {}, {}, {}, {}

    def cell(i):
        u = value(i)
        v = speed(i)
        if kind == 0:
            f = u * v
        elif kind == 1:
            f = u * v + extra(i)
        else:
            f = (u + extra(i)) * v
        us[i], fs[i] = u, f

    def diff(i):
        cell(i + 1)
        du[i] = us[i + 1] - us[i]
        df[i] = fs[i + 1] - fs[i]

    cell(lo - 2)
    for i in range(lo - 2, lo + 2):
        diff(i)
    head = None
    for j in range(lo, hi + 1):
        diff(j + 2)
        now = face(
            fs[j] + fs[j + 1],
            alpha(j),
            [df[j + k] for k in range(-2, 3)],
            [du[j + k] for k in range(-2, 3)],
        )
        head = now if head is None else head
        if before is not None:
            emit(j, now - before)
        before = now
    if after is not None:
        emit(hi + 1, after - before)
    return head, before


def widest(m):
    return jnp.maximum(jnp.maximum(jnp.maximum(m[0], m[1]), jnp.maximum(m[2], m[3])), jnp.maximum(m[4], m[5]))


def step_kernel(
    sizes,
    start, fresh, third,
    first, second, acc, accy, accz, turned, ends,
    xlo, xhi, ylo, yhi, ysl, ysh, zu,
    nat, xt, yt, zt, ax, ay, az,
    send, recv,
):
    n_tube, n_gy, n_gz = sizes
    me_t, me_y, me_z = lax.axis_index("tube"), lax.axis_index("gy"), lax.axis_index("gz")
    has_lo, has_hi = me_t > 0, me_t < n_tube - 1
    y_next, y_prev = lax.rem(me_y + 1, n_gy), lax.rem(me_y + n_gy - 1, n_gy)
    z_next, z_prev = lax.rem(me_z + 1, n_gz), lax.rem(me_z + n_gz - 1, n_gz)

    def to(tube=None, gy=None, gz=None):
        return (
            me_t if tube is None else tube,
            me_y if gy is None else gy,
            me_z if gz is None else gz,
        )

    barrier = pltpu.get_barrier_semaphore()
    for there in (to(gy=y_next), to(gy=y_prev), to(gz=z_next), to(gz=z_prev)):
        pl.semaphore_signal(barrier, inc=1, device_id=there, device_id_type=MESH)

    @pl.when(has_lo)
    def _():
        pl.semaphore_signal(barrier, inc=1, device_id=to(tube=me_t - 1), device_id_type=MESH)

    @pl.when(has_hi)
    def _():
        pl.semaphore_signal(barrier, inc=1, device_id=to(tube=me_t + 1), device_id_type=MESH)

    pl.semaphore_wait(barrier, 4 + lax.min(me_t, 1) + lax.min(n_tube - 1 - me_t, 1))

    def remote(src, dst, stage, slot, there):
        return pltpu.make_async_remote_copy(
            src_ref=src, dst_ref=dst, send_sem=send.at[stage, slot], recv_sem=recv.at[stage, slot],
            device_id=there, device_id_type=MESH,
        )

    def copies(stage, cur):
        x_up = remote(cur.at[:, pl.ds(0, 24), :], xhi.at[stage], stage, 0, to(tube=me_t - 1))
        x_down = remote(cur.at[:, pl.ds(104, 24), :], xlo.at[stage], stage, 1, to(tube=me_t + 1))
        y_up = remote(ysh.at[stage], ylo.at[stage], stage, 2, to(gy=y_next))
        y_down = remote(ysl.at[stage], yhi.at[stage], stage, 3, to(gy=y_prev))
        z_up = remote(
            zu.at[stage, :, pl.ds(128, 8), :], zu.at[stage, :, pl.ds(0, 8), :], stage, 4, to(gz=z_next)
        )
        z_down = remote(
            zu.at[stage, :, pl.ds(8, 8), :], zu.at[stage, :, pl.ds(136, 8), :], stage, 5, to(gz=z_prev)
        )
        return x_up, x_down, y_up, y_down, z_up, z_down

    def plane(ref, p):
        return ref[pl.ds(8 * p, 8), :]

    def regular(d, body):
        @pl.loop(0, 11)
        def _(k):
            body(k + (k + 7 - d) // 16, 0)

        body(9 + d, 1)
        body(12, 2)

    def stage_step(stage, cur, out, a, b):
        x_up, x_down, y_up, y_down, z_up, z_down = copies(stage, cur)

        z_up.start()
        z_down.start()

        @pl.when(has_lo)
        def _():
            x_up.start()

        @pl.when(has_hi)
        def _():
            x_down.start()

        @pl.loop(0, 13)
        def _(c):
            for k in range(3):
                for g in range(2):
                    ysl[stage, c, 2 * k + g] = cur[c, pl.ds(64 * g + k, 8, stride=8), :]
                    ysh[stage, c, 2 * k + g] = cur[c, pl.ds(64 * g + 5 + k, 8, stride=8), :]

        y_up.start()
        y_down.start()

        @pl.loop(0, 8)
        def _(q):
            for h in range(2):
                rows = pl.ds(pl.multiple_of(16 * q + 8 * h, 8), 8)
                u = [cur[c, rows, :] for c in range(13)]
                r, pressure, sound = gas(u)
                nat[0, rows, :] = pressure
                for d in range(3):
                    v = u[9 + d] * r
                    nat[1 + d, rows, :] = v
                    nat[4 + d, rows, :] = jnp.abs(v) + sound

        zt[0, pl.ds(8, 128), :] = jnp.transpose(nat[0])
        zt[1, pl.ds(8, 128), :] = jnp.transpose(nat[3])
        zt[2, pl.ds(8, 128), :] = jnp.transpose(nat[6])

        def x_value(c, i):
            if i < 0:
                return xlo[stage, c, pl.ds(8 * (i + 3), 8), :]
            if i > 15:
                return xhi[stage, c, pl.ds(8 * (i - 16), 8), :]
            return cur[c, pl.ds(8 * i, 8), :]

        def x_of(row, nat_row, i):
            if i < 0:
                return xt[row, i + 3]
            if i > 15:
                return xt[row, i - 13]
            return nat[nat_row, pl.ds(8 * i, 8), :]

        def x_alpha(j):
            ax[j + 1] = widest([x_of(2, 4, j + k) for k in range(-2, 4)])

        def x_sweep(c, kind, lo, hi, **known):
            def emit(i, change):
                rows = pl.ds(8 * i, 8)
                acc[c, rows, :] = change

            return sweep(
                lo, hi, lambda i: x_value(c, i), lambda i: x_of(1, 1, i), lambda i: x_of(0, 0, i),
                kind, lambda j: ax[j + 1], emit, **known,
            )

        for j in range(2, 13):
            x_alpha(j)

        def x_inner(c, kind):
            ends[c, 0], ends[c, 1] = x_sweep(c, kind, 2, 12)

        regular(0, x_inner)

        z_up.wait_recv()
        z_down.wait_recv()
        for h in range(2):
            rows = pl.ds(136 * h, 8)
            r, pressure, sound = gas([zu[stage, c, rows, :] for c in range(13)])
            v = zu[stage, 11, rows, :] * r
            zt[0, rows, :] = pressure
            zt[1, rows, :] = v
            zt[2, rows, :] = jnp.abs(v) + sound

        def z_rows(i):
            return pl.ds(8 + i, 8, stride=16)

        for j in range(-1, 16):
            az[j + 1] = widest([zt[2, z_rows(j + k), :] for k in range(-2, 4)])

        def z_body(c, kind):
            def emit(i, change):
                accz[c, pl.ds(i, 8, stride=16), :] = change

            sweep(
                -1, 15, lambda i: zu[stage, c, z_rows(i), :], lambda i: zt[1, z_rows(i), :],
                lambda i: zt[0, z_rows(i), :], kind, lambda j: az[j + 1], emit,
            )

        regular(2, z_body)

        @pl.when(has_lo)
        def _():
            x_down.wait_recv()

        @pl.when(has_hi)
        def _():
            x_up.wait_recv()

        @pl.when(jnp.logical_not(has_lo))
        def _():
            @pl.loop(0, 13)
            def _(c):
                for k in range(3):
                    xlo[stage, c, pl.ds(8 * k, 8), :] = cur[c, pl.ds(0, 8), :]

        @pl.when(jnp.logical_not(has_hi))
        def _():
            @pl.loop(0, 13)
            def _(c):
                for k in range(3):
                    xhi[stage, c, pl.ds(8 * k, 8), :] = fresh[c]

        for i in (-3, -2, -1, 16, 17, 18):
            u = [x_value(c, i) for c in range(13)]
            r, pressure, sound = gas(u)
            v = u[9] * r
            k = i + 3 if i < 0 else i - 13
            xt[0, k] = pressure
            xt[1, k] = v
            xt[2, k] = jnp.abs(v) + sound

        for j in (-1, 0, 1, 13, 14, 15):
            x_alpha(j)

        def x_outer(c, kind):
            x_sweep(c, kind, -1, 1, after=ends[c, 0])
            x_sweep(c, kind, 13, 15, before=ends[c, 1])
            turned[c] = jnp.transpose(accz[c])

        regular(0, x_outer)

        y_up.wait_recv()
        y_down.wait_recv()

        def y_value(c, g, i):
            if i < 0:
                return ylo[stage, c, 2 * (i + 3) + g]
            if i > 7:
                return yhi[stage, c, 2 * (i - 8) + g]
            return cur[c, pl.ds(64 * g + i, 8, stride=8), :]

        for g in range(2):
            for i in range(-3, 11):
                k = 2 * (i + 3) + g
                if 0 <= i < 8:
                    for row, nat_row in ((0, 0), (1, 2), (2, 5)):
                        yt[row, k] = nat[nat_row, pl.ds(64 * g + i, 8, stride=8), :]
                else:
                    u = [y_value(c, g, i) for c in range(13)]
                    r, pressure, sound = gas(u)
                    v = u[10] * r
                    yt[0, k] = pressure
                    yt[1, k] = v
                    yt[2, k] = jnp.abs(v) + sound
            for j in range(-1, 8):
                ay[2 * (j + 1) + g] = widest([yt[2, 2 * (j + k + 3) + g] for k in range(-2, 4)])

        def y_body(c, kind):
            for g in range(2):
                def emit(i, change):
                    accy[c, pl.ds(16 * i + 8 * g, 8), :] = change

                sweep(
                    -1, 7, lambda i: y_value(c, g, i), lambda i: yt[1, 2 * (i + 3) + g],
                    lambda i: yt[0, 2 * (i + 3) + g], kind, lambda j: ay[2 * (j + 1) + g], emit,
                )

        regular(1, y_body)

        for c in range(13):
            across = [accy[c, pl.ds(8 * (p // 8) + p % 8, 8, stride=16), :] for p in range(16)]
            change = acc[c] + turned[c] + jnp.concatenate(across, axis=0)
            moved = b * cur[c] - (b * DT / 12.0) * change
            if a != 0.0:
                moved = a * start[c] + moved
            out[c] = moved
            if stage < 2:
                zu[stage + 1, c, pl.ds(8, 128), :] = jnp.transpose(moved)

    for c in range(13):
        zu[0, c, pl.ds(8, 128), :] = jnp.transpose(start[c])
    stage_step(0, start, first, 0.0, 1.0)
    stage_step(1, first, second, 0.75, 0.25)
    stage_step(2, second, third, 1.0 / 3.0, 2.0 / 3.0)

    for stage, cur in enumerate((start, first, second)):
        x_up, x_down, y_up, y_down, z_up, z_down = copies(stage, cur)
        for copy in (y_up, y_down, z_up, z_down):
            copy.wait_send()

        @pl.when(has_lo)
        def _():
            x_up.wait_send()

        @pl.when(has_hi)
        def _():
            x_down.wait_send()


def advance_flow(start, fresh, sizes):
    tile = (8, 128)
    vmem = pl.BlockSpec(memory_space=pltpu.VMEM)
    scratch = [
        pltpu.VMEM((13, 128, 128), F32),
        pltpu.VMEM((13, 128, 128), F32),
        pltpu.VMEM((13, 128, 128), F32),
        pltpu.VMEM((13, 128, 128), F32),
        pltpu.VMEM((13, 128, 128), F32),
        pltpu.VMEM((13, 128, 128), F32),
        pltpu.VMEM((13, 2) + tile, F32),
        pltpu.VMEM((3, 13, 24, 128), F32),
        pltpu.VMEM((3, 13, 24, 128), F32),
        pltpu.VMEM((3, 13, 6) + tile, F32),
        pltpu.VMEM((3, 13, 6) + tile, F32),
        pltpu.VMEM((3, 13, 6) + tile, F32),
        pltpu.VMEM((3, 13, 6) + tile, F32),
        pltpu.VMEM((3, 13, 144, 128), F32),
        pltpu.VMEM((7, 128, 128), F32),
        pltpu.VMEM((3, 6) + tile, F32),
        pltpu.VMEM((3, 28) + tile, F32),
        pltpu.VMEM((3, 144, 128), F32),
        pltpu.VMEM((17,) + tile, F32),
        pltpu.VMEM((18,) + tile, F32),
        pltpu.VMEM((17,) + tile, F32),
        pltpu.SemaphoreType.DMA((3, 6)),
        pltpu.SemaphoreType.DMA((3, 6)),
    ]
    return pl.pallas_call(
        functools.partial(step_kernel, sizes),
        out_shape=jax.ShapeDtypeStruct((13, 128, 128), F32),
        in_specs=[vmem, vmem],
        out_specs=vmem,
        scratch_shapes=scratch,
        compiler_params=pltpu.CompilerParams(collective_id=0, has_side_effects=True),
        name="flow",
    )(start, fresh)


def rates(c, y):
    h = jnp.exp(-0.5 * y)
    g = jnp.exp(-0.3 * y)
    e1 = h * h
    e15 = e1 * h
    e3 = e15 * e15
    e4 = e3 * e1
    e45 = e3 * e15
    e5 = e4 * e1
    e6 = e3 * e3
    e08 = h * g
    c31 = c[3] * c[1]
    c45 = c[4] * c[5]
    c40 = c[4] * c[0]
    c35 = c[3] * c[5]
    n0 = 30.0 * e4 * c31 - 8.0 * e1 * c45
    n2 = 20.0 * e3 * c40 - 6.0 * e15 * c35
    n4 = 25.0 * e15 * (c[0] * c[5]) - 10.0 * e45 * (c[2] * c[3])
    n6 = 12.0 * e4 * (c[4] * c[2]) - 5.0 * e15 * (c[5] * c[5])
    r8 = 4.0 * e6 * (c[0] * c[8])
    third = h * c[8]
    c34 = c[3] * c[4]
    r9 = 20.0 * third * (c[3] * c[3])
    r10 = 15.0 * third * (c[4] * c[4])
    r11 = 18.0 * third * c34
    r12 = 22.0 * third * c35
    r13 = 25.0 * (g * c[8]) * c31
    c63 = c[6] * c[3]
    r14 = 30.0 * e08 * c63
    r15 = 25.0 * h * c63
    r16 = 20.0 * g * (c[6] * c[4])
    r17 = 30.0 * g * (c[6] * c[5])
    r18 = 10.0 * h * (c[6] * c[6])
    r19 = 6.0 * e5 * (c[7] * c[8])
    r20 = 15.0 * e15 * (c[7] * c[3])
    s89 = r8 - r9
    a1113 = r11 + r13
    a1415 = r14 + r15
    a1617 = r16 + r17
    w = [None] * 9
    w[0] = (r14 - n2) - (n4 + s89)
    w[1] = (r10 - n0) + (r14 - r13) + (a1617 + r18)
    w[2] = (n4 - n6) + (r12 + r17) + r20
    w[3] = (n2 - n0) + (n4 + (s89 + s89)) - (a1113 + r12) - (a1415 + r20)
    w[4] = (n0 - n2) - n6 - (r10 + r10) - (r11 + r16)
    two = n6 + r15 + r19
    w[5] = (n0 + n2) - n4 + (two + two) + (r11 - r12) + (r16 - r17) + r20
    w[6] = r13 - (a1415 + a1617) - (r18 + r18)
    w[7] = r18 - (r19 + r20)
    w[8] = -((r8 + r9) + (r10 + r12) + (a1113 + r19))
    return w


def react_kernel(planes, u_ref, n_ref, o_ref):
    def block(q, _):
        rows = [pl.ds(pl.multiple_of(8 * planes * q + 8 * h, 8), 8) for h in range(planes)]
        for row in rows:
            for k in range(9, 13):
                o_ref[k, row, :] = u_ref[k, row, :]
        state = []
        fixed = []
        for row in rows:
            u = [u_ref[k, row, :] for k in range(13)]
            rho = total(u[:9])
            internal = u[12] - 0.5 * (u[9] * u[9] + u[10] * u[10] + u[11] * u[11]) / rho
            counts = n_ref[row, :]
            fixed.append((internal, counts, DT / counts.astype(F32)))
            state.append(tuple(u[k] * IW[k] for k in range(9)))

        def substep(i, state):
            new = []
            for c, (internal, counts, step) in zip(state, fixed):
                s1 = total([c[0], c[1], c[5], c[8]])
                s2 = total([c[2], c[6], c[7]])
                heat = 2.5 * s1 + 3.0 * s2 + 1.5 * (c[3] + c[4])
                bound = total([
                    (-1.5 * W[2]) * c[2], (12.0 * W[3]) * c[3], (1.5 * W[4]) * c[4],
                    (0.25 * W[5]) * c[5], (0.02 * W[6]) * c[6], (-0.45 * W[7]) * c[7],
                ])
                w = rates(c, heat / (internal - bound))
                live = i < counts
                new.append(tuple(jnp.where(live, c[k] + step * w[k], c[k]) for k in range(9)))
            return tuple(new)

        state = lax.fori_loop(0, CMAX, substep, tuple(state))
        for row, c in zip(rows, state):
            for k in range(9):
                o_ref[k, row, :] = c[k] * W[k]
        return 0

    lax.fori_loop(0, u_ref.shape[1] // (8 * planes), block, 0)


def react(third, substeps):
    steps = 4
    size = 128 // steps
    return pl.pallas_call(
        functools.partial(react_kernel, 2),
        out_shape=jax.ShapeDtypeStruct((13, 128, 128), F32),
        grid=(steps,),
        in_specs=[
            pl.BlockSpec((13, size, 128), lambda i: (0, i, 0)),
            pl.BlockSpec((size, 128), lambda i: (i, 0)),
        ],
        out_specs=pl.BlockSpec((13, size, 128), lambda i: (0, i, 0)),
        name="react",
    )(third, substeps)


def on_device(sizes, state, fresh, substeps, shift):
    comps, planes, wy, wz = state.shape
    n_tube = sizes[0]
    ahead = lax.ppermute(state[:, :SMAX], "tube", [(i, i - 1) for i in range(1, n_tube)])
    joined = jnp.concatenate([state, ahead], axis=1)
    start = lax.dynamic_slice_in_dim(joined, shift, planes, 1)
    position = lax.axis_index("tube") * planes + lax.iota(jnp.int32, planes)
    beyond = (position + shift >= n_tube * planes)[None, :, None, None]
    start = jnp.where(beyond, fresh[:, None], start)
    third = advance_flow(start.reshape(comps, planes * wy, wz), fresh, sizes)
    out = react(third, substeps.reshape(planes * wy, wz))
    return out.reshape(comps, planes, wy, wz)


def solution(mesh):
    sizes = tuple(mesh.shape[name] for name in ("tube", "gy", "gz"))
    return jax.shard_map(
        functools.partial(on_device, sizes),
        mesh=mesh,
        in_specs=(P(None, "tube", "gy", "gz"), P(None, "gy", "gz"), P("tube", "gy", "gz"), P()),
        out_specs=P(None, "tube", "gy", "gz"),
        check_vma=False,
    )
```

```python
import functools

import jax
import jax.numpy as jnp
import numpy as np
from jax import lax
from jax.experimental import pallas as pl
from jax.experimental.pallas import tpu as pltpu
from jax.sharding import PartitionSpec as P

SMAX = 12
CMAX = 8
DT = 0.05
W = [float(w) for w in np.array([2.016, 31.998, 18.015, 1.008, 15.999, 17.007, 33.006, 34.014, 28.014]) / 18.015]
IW = [1.0 / w for w in W]
MESH = pl.DeviceIdType.MESH
F32 = jnp.float32


def total(parts):
    while len(parts) > 1:
        parts = [a + b for a, b in zip(parts[::2], parts[1::2])] + ([parts[-1]] if len(parts) % 2 else [])
    return parts[0]


def gas(u):
    rho = total(list(u[:9]))
    c = [u[k] * IW[k] for k in range(9)]
    s1 = total([c[0], c[1], c[5], c[8]])
    s2 = total([c[2], c[6], c[7]])
    s3 = c[3] + c[4]
    gas_sum = s1 + s2 + s3
    heat = 2.5 * s1 + 3.0 * s2 + 1.5 * s3
    bound = total([-1.5 * u[2], 12.0 * u[3], 1.5 * u[4], 0.25 * u[5], 0.02 * u[6], -0.45 * u[7]])
    r = 1.0 / rho
    kinetic = 0.5 * r * (u[9] * u[9] + u[10] * u[10] + u[11] * u[11])
    over = 1.0 / heat
    pressure = gas_sum * ((u[12] - kinetic - bound) * over)
    sound = jnp.sqrt((1.0 + gas_sum * over) * pressure * r)
    return r, pressure, sound


def one_side(e1, e2, e3, e4):
    k2 = e2 * e2 * 0.609375 + 3e-6
    k3 = e3 * e3 * 0.609375 + 3e-6
    ta = e1 - 1.375 * e2
    tb = e3 - 0.625 * e2
    tc = e4 - 1.375 * e3
    ra = 1.0 / (ta * ta + k2)
    rb = 1.0 / (tb * tb + k2)
    rc = 1.0 / (tc * tc + k3)
    d23 = e3 - e2
    a = ta + tb
    c = d23 - (e4 - e3)
    wa = ra * ra
    wb = rb * rb * 6.0
    wc = rc * rc * 3.0
    return (wc * c - wa * (a + a)) / (wa + wb + wc) - d23


def face(pair_sum, alpha, df, du):
    p = [alpha * d for d in du]
    plus = [df[k] + p[k] for k in range(4)]
    minus = [df[k] - p[k] for k in range(1, 5)]
    x = one_side(plus[0], plus[1], plus[2], plus[3])
    y = one_side(minus[3], minus[2], minus[1], minus[0])
    return 6.0 * pair_sum + (x - y)


def sweep(lo, hi, value, speed, extra, kind, alpha, emit, before=None, after=None):
    us, fs, du, df = {}, {}, {}, {}

    def cell(i):
        u = value(i)
        v = speed(i)
        if kind == 0:
            f = u * v
        elif kind == 1:
            f = u * v + extra(i)
        else:
            f = (u + extra(i)) * v
        us[i], fs[i] = u, f

    def diff(i):
        cell(i + 1)
        du[i] = us[i + 1] - us[i]
        df[i] = fs[i + 1] - fs[i]

    cell(lo - 2)
    for i in range(lo - 2, lo + 2):
        diff(i)
    head = None
    for j in range(lo, hi + 1):
        diff(j + 2)
        now = face(
            fs[j] + fs[j + 1],
            alpha(j),
            [df[j + k] for k in range(-2, 3)],
            [du[j + k] for k in range(-2, 3)],
        )
        head = now if head is None else head
        if before is not None:
            emit(j, now - before)
        before = now
    if after is not None:
        emit(hi + 1, after - before)
    return head, before


def widest(m):
    return jnp.maximum(jnp.maximum(jnp.maximum(m[0], m[1]), jnp.maximum(m[2], m[3])), jnp.maximum(m[4], m[5]))


def step_kernel(
    sizes,
    start, fresh, third,
    first, second, acc, accy, accz, turned, ends,
    xlo, xhi, ylo, yhi, ysl, ysh, zu,
    nat, xt, yt, zt, ax, ay, az,
    send, recv,
):
    n_tube, n_gy, n_gz = sizes
    me_t, me_y, me_z = lax.axis_index("tube"), lax.axis_index("gy"), lax.axis_index("gz")
    has_lo, has_hi = me_t > 0, me_t < n_tube - 1
    y_next, y_prev = lax.rem(me_y + 1, n_gy), lax.rem(me_y + n_gy - 1, n_gy)
    z_next, z_prev = lax.rem(me_z + 1, n_gz), lax.rem(me_z + n_gz - 1, n_gz)

    def to(tube=None, gy=None, gz=None):
        return (
            me_t if tube is None else tube,
            me_y if gy is None else gy,
            me_z if gz is None else gz,
        )

    barrier = pltpu.get_barrier_semaphore()
    for there in (to(gy=y_next), to(gy=y_prev), to(gz=z_next), to(gz=z_prev)):
        pl.semaphore_signal(barrier, inc=1, device_id=there, device_id_type=MESH)

    @pl.when(has_lo)
    def _():
        pl.semaphore_signal(barrier, inc=1, device_id=to(tube=me_t - 1), device_id_type=MESH)

    @pl.when(has_hi)
    def _():
        pl.semaphore_signal(barrier, inc=1, device_id=to(tube=me_t + 1), device_id_type=MESH)

    pl.semaphore_wait(barrier, 4 + lax.min(me_t, 1) + lax.min(n_tube - 1 - me_t, 1))

    def remote(src, dst, stage, slot, there):
        return pltpu.make_async_remote_copy(
            src_ref=src, dst_ref=dst, send_sem=send.at[stage, slot], recv_sem=recv.at[stage, slot],
            device_id=there, device_id_type=MESH,
        )

    def copies(stage, cur):
        x_up = remote(cur.at[:, pl.ds(0, 24), :], xhi.at[stage], stage, 0, to(tube=me_t - 1))
        x_down = remote(cur.at[:, pl.ds(104, 24), :], xlo.at[stage], stage, 1, to(tube=me_t + 1))
        y_up = remote(ysh.at[stage], ylo.at[stage], stage, 2, to(gy=y_next))
        y_down = remote(ysl.at[stage], yhi.at[stage], stage, 3, to(gy=y_prev))
        z_up = remote(
            zu.at[stage, :, pl.ds(128, 8), :], zu.at[stage, :, pl.ds(0, 8), :], stage, 4, to(gz=z_next)
        )
        z_down = remote(
            zu.at[stage, :, pl.ds(8, 8), :], zu.at[stage, :, pl.ds(136, 8), :], stage, 5, to(gz=z_prev)
        )
        return x_up, x_down, y_up, y_down, z_up, z_down

    def pack(stage, cur, c):
        zu[stage, c, pl.ds(8, 128), :] = jnp.transpose(cur[c])
        for k in range(3):
            for g in range(2):
                ysl[stage, c, 2 * k + g] = cur[c, pl.ds(64 * g + k, 8, stride=8), :]
                ysh[stage, c, 2 * k + g] = cur[c, pl.ds(64 * g + 5 + k, 8, stride=8), :]

    def launch(stage, cur, c):
        low, high = pl.ds(8, 8), pl.ds(128, 8)
        remote(zu.at[stage, c, high, :], zu.at[stage, c, pl.ds(0, 8), :], stage, 4, to(gz=z_next)).start()
        remote(zu.at[stage, c, low, :], zu.at[stage, c, pl.ds(136, 8), :], stage, 5, to(gz=z_prev)).start()

        @pl.when(has_lo)
        def _():
            remote(cur.at[c, pl.ds(0, 24), :], xhi.at[stage, c], stage, 0, to(tube=me_t - 1)).start()

        @pl.when(has_hi)
        def _():
            remote(cur.at[c, pl.ds(104, 24), :], xlo.at[stage, c], stage, 1, to(tube=me_t + 1)).start()

        remote(ysh.at[stage, c], ylo.at[stage, c], stage, 2, to(gy=y_next)).start()
        remote(ysl.at[stage, c], yhi.at[stage, c], stage, 3, to(gy=y_prev)).start()

    def regular(d, body):
        @pl.loop(0, 11)
        def _(k):
            body(k + (k + 7 - d) // 16, 0)

        body(9 + d, 1)
        body(12, 2)

    def stage_step(stage, cur, out, a, b):
        x_up, x_down, y_up, y_down, z_up, z_down = copies(stage, cur)

        @pl.loop(0, 8)
        def _(q):
            for h in range(2):
                rows = pl.ds(pl.multiple_of(16 * q + 8 * h, 8), 8)
                u = [cur[c, rows, :] for c in range(13)]
                r, pressure, sound = gas(u)
                nat[0, rows, :] = pressure
                for d in range(3):
                    v = u[9 + d] * r
                    nat[1 + d, rows, :] = v
                    nat[4 + d, rows, :] = jnp.abs(v) + sound

        zt[0, pl.ds(8, 128), :] = jnp.transpose(nat[0])
        zt[1, pl.ds(8, 128), :] = jnp.transpose(nat[3])
        zt[2, pl.ds(8, 128), :] = jnp.transpose(nat[6])

        def x_value(c, i):
            if i < 0:
                return xlo[stage, c, pl.ds(8 * (i + 3), 8), :]
            if i > 15:
                return xhi[stage, c, pl.ds(8 * (i - 16), 8), :]
            return cur[c, pl.ds(8 * i, 8), :]

        def x_of(row, nat_row, i):
            if i < 0:
                return xt[row, i + 3]
            if i > 15:
                return xt[row, i - 13]
            return nat[nat_row, pl.ds(8 * i, 8), :]

        def x_alpha(j):
            ax[j + 1] = widest([x_of(2, 4, j + k) for k in range(-2, 4)])

        def x_sweep(c, kind, lo, hi, **known):
            def emit(i, change):
                rows = pl.ds(8 * i, 8)
                acc[c, rows, :] = change

            return sweep(
                lo, hi, lambda i: x_value(c, i), lambda i: x_of(1, 1, i), lambda i: x_of(0, 0, i),
                kind, lambda j: ax[j + 1], emit, **known,
            )

        for j in range(2, 13):
            x_alpha(j)

        def x_inner(c, kind):
            ends[c, 0], ends[c, 1] = x_sweep(c, kind, 2, 12)

        regular(0, x_inner)

        z_up.wait_recv()
        z_down.wait_recv()
        for h in range(2):
            rows = pl.ds(136 * h, 8)
            r, pressure, sound = gas([zu[stage, c, rows, :] for c in range(13)])
            v = zu[stage, 11, rows, :] * r
            zt[0, rows, :] = pressure
            zt[1, rows, :] = v
            zt[2, rows, :] = jnp.abs(v) + sound

        def z_rows(i):
            return pl.ds(8 + i, 8, stride=16)

        for j in range(-1, 16):
            az[j + 1] = widest([zt[2, z_rows(j + k), :] for k in range(-2, 4)])

        def z_body(c, kind):
            def emit(i, change):
                accz[c, pl.ds(i, 8, stride=16), :] = change

            sweep(
                -1, 15, lambda i: zu[stage, c, z_rows(i), :], lambda i: zt[1, z_rows(i), :],
                lambda i: zt[0, z_rows(i), :], kind, lambda j: az[j + 1], emit,
            )

        regular(2, z_body)

        @pl.when(has_lo)
        def _():
            x_down.wait_recv()

        @pl.when(has_hi)
        def _():
            x_up.wait_recv()

        @pl.when(jnp.logical_not(has_lo))
        def _():
            @pl.loop(0, 13)
            def _(c):
                for k in range(3):
                    xlo[stage, c, pl.ds(8 * k, 8), :] = cur[c, pl.ds(0, 8), :]

        @pl.when(jnp.logical_not(has_hi))
        def _():
            @pl.loop(0, 13)
            def _(c):
                for k in range(3):
                    xhi[stage, c, pl.ds(8 * k, 8), :] = fresh[c]

        for i in (-3, -2, -1, 16, 17, 18):
            u = [x_value(c, i) for c in range(13)]
            r, pressure, sound = gas(u)
            v = u[9] * r
            k = i + 3 if i < 0 else i - 13
            xt[0, k] = pressure
            xt[1, k] = v
            xt[2, k] = jnp.abs(v) + sound

        for j in (-1, 0, 1, 13, 14, 15):
            x_alpha(j)

        def x_outer(c, kind):
            x_sweep(c, kind, -1, 1, after=ends[c, 0])
            x_sweep(c, kind, 13, 15, before=ends[c, 1])
            turned[c] = jnp.transpose(accz[c])

        regular(0, x_outer)

        y_up.wait_recv()
        y_down.wait_recv()

        def y_value(c, g, i):
            if i < 0:
                return ylo[stage, c, 2 * (i + 3) + g]
            if i > 7:
                return yhi[stage, c, 2 * (i - 8) + g]
            return cur[c, pl.ds(64 * g + i, 8, stride=8), :]

        for g in range(2):
            for i in range(-3, 11):
                k = 2 * (i + 3) + g
                if 0 <= i < 8:
                    for row, nat_row in ((0, 0), (1, 2), (2, 5)):
                        yt[row, k] = nat[nat_row, pl.ds(64 * g + i, 8, stride=8), :]
                else:
                    u = [y_value(c, g, i) for c in range(13)]
                    r, pressure, sound = gas(u)
                    v = u[10] * r
                    yt[0, k] = pressure
                    yt[1, k] = v
                    yt[2, k] = jnp.abs(v) + sound
            for j in range(-1, 8):
                ay[2 * (j + 1) + g] = widest([yt[2, 2 * (j + k + 3) + g] for k in range(-2, 4)])

        def y_body(c, kind):
            for g in range(2):
                def emit(i, change):
                    accy[c, pl.ds(16 * i + 8 * g, 8), :] = change

                sweep(
                    -1, 7, lambda i: y_value(c, g, i), lambda i: yt[1, 2 * (i + 3) + g],
                    lambda i: yt[0, 2 * (i + 3) + g], kind, lambda j: ay[2 * (j + 1) + g], emit,
                )

        def update(c):
            across = [accy[c, pl.ds(8 * (p // 8) + p % 8, 8, stride=16), :] for p in range(16)]
            change = acc[c] + turned[c] + jnp.concatenate(across, axis=0)
            moved = b * cur[c] - (b * DT / 12.0) * change
            if a != 0.0:
                moved = a * start[c] + moved
            out[c] = moved
            if stage < 2:
                pack(stage + 1, out, c)

        def send_on(c):
            if stage < 2:
                launch(stage + 1, out, c)

        def order(k):
            return k + (k + 6) // 16

        y_body(0, 0)

        @pl.loop(1, 11)
        def _(k):
            if stage < 2:
                @pl.when(k > 1)
                def _():
                    send_on(order(k - 2))

            update(order(k - 1))
            y_body(order(k), 0)

        send_on(9)
        update(11)
        y_body(10, 1)
        send_on(11)
        update(10)
        y_body(12, 2)
        send_on(10)
        update(12)
        send_on(12)

    @pl.loop(0, 13)
    def _(c):
        @pl.when(c > 0)
        def _():
            launch(0, start, c - 1)

        pack(0, start, c)

    launch(0, start, 12)
    stage_step(0, start, first, 0.0, 1.0)
    stage_step(1, first, second, 0.75, 0.25)
    stage_step(2, second, third, 1.0 / 3.0, 2.0 / 3.0)

    for stage, cur in enumerate((start, first, second)):
        x_up, x_down, y_up, y_down, z_up, z_down = copies(stage, cur)
        for copy in (y_up, y_down, z_up, z_down):
            copy.wait_send()

        @pl.when(has_lo)
        def _():
            x_up.wait_send()

        @pl.when(has_hi)
        def _():
            x_down.wait_send()


def advance_flow(start, fresh, sizes):
    tile = (8, 128)
    vmem = pl.BlockSpec(memory_space=pltpu.VMEM)
    scratch = [
        pltpu.VMEM((13, 128, 128), F32),
        pltpu.VMEM((13, 128, 128), F32),
        pltpu.VMEM((13, 128, 128), F32),
        pltpu.VMEM((13, 128, 128), F32),
        pltpu.VMEM((13, 128, 128), F32),
        pltpu.VMEM((13, 128, 128), F32),
        pltpu.VMEM((13, 2) + tile, F32),
        pltpu.VMEM((3, 13, 24, 128), F32),
        pltpu.VMEM((3, 13, 24, 128), F32),
        pltpu.VMEM((3, 13, 6) + tile, F32),
        pltpu.VMEM((3, 13, 6) + tile, F32),
        pltpu.VMEM((3, 13, 6) + tile, F32),
        pltpu.VMEM((3, 13, 6) + tile, F32),
        pltpu.VMEM((3, 13, 144, 128), F32),
        pltpu.VMEM((7, 128, 128), F32),
        pltpu.VMEM((3, 6) + tile, F32),
        pltpu.VMEM((3, 28) + tile, F32),
        pltpu.VMEM((3, 144, 128), F32),
        pltpu.VMEM((17,) + tile, F32),
        pltpu.VMEM((18,) + tile, F32),
        pltpu.VMEM((17,) + tile, F32),
        pltpu.SemaphoreType.DMA((3, 6)),
        pltpu.SemaphoreType.DMA((3, 6)),
    ]
    return pl.pallas_call(
        functools.partial(step_kernel, sizes),
        out_shape=jax.ShapeDtypeStruct((13, 128, 128), F32),
        in_specs=[vmem, vmem],
        out_specs=vmem,
        scratch_shapes=scratch,
        compiler_params=pltpu.CompilerParams(collective_id=0, has_side_effects=True),
        name="flow",
    )(start, fresh)


def rates(c, y):
    h = jnp.exp(-0.5 * y)
    g = jnp.exp(-0.3 * y)
    e1 = h * h
    e15 = e1 * h
    e3 = e15 * e15
    e4 = e3 * e1
    e45 = e3 * e15
    e5 = e4 * e1
    e6 = e3 * e3
    e08 = h * g
    c31 = c[3] * c[1]
    c45 = c[4] * c[5]
    c40 = c[4] * c[0]
    c35 = c[3] * c[5]
    n0 = 30.0 * e4 * c31 - 8.0 * e1 * c45
    n2 = 20.0 * e3 * c40 - 6.0 * e15 * c35
    n4 = 25.0 * e15 * (c[0] * c[5]) - 10.0 * e45 * (c[2] * c[3])
    n6 = 12.0 * e4 * (c[4] * c[2]) - 5.0 * e15 * (c[5] * c[5])
    r8 = 4.0 * e6 * (c[0] * c[8])
    third = h * c[8]
    c34 = c[3] * c[4]
    r9 = 20.0 * third * (c[3] * c[3])
    r10 = 15.0 * third * (c[4] * c[4])
    r11 = 18.0 * third * c34
    r12 = 22.0 * third * c35
    r13 = 25.0 * (g * c[8]) * c31
    c63 = c[6] * c[3]
    r14 = 30.0 * e08 * c63
    r15 = 25.0 * h * c63
    r16 = 20.0 * g * (c[6] * c[4])
    r17 = 30.0 * g * (c[6] * c[5])
    r18 = 10.0 * h * (c[6] * c[6])
    r19 = 6.0 * e5 * (c[7] * c[8])
    r20 = 15.0 * e15 * (c[7] * c[3])
    s89 = r8 - r9
    a1113 = r11 + r13
    a1415 = r14 + r15
    a1617 = r16 + r17
    w = [None] * 9
    w[0] = (r14 - n2) - (n4 + s89)
    w[1] = (r10 - n0) + (r14 - r13) + (a1617 + r18)
    w[2] = (n4 - n6) + (r12 + r17) + r20
    w[3] = (n2 - n0) + (n4 + (s89 + s89)) - (a1113 + r12) - (a1415 + r20)
    w[4] = (n0 - n2) - n6 - (r10 + r10) - (r11 + r16)
    two = n6 + r15 + r19
    w[5] = (n0 + n2) - n4 + (two + two) + (r11 - r12) + (r16 - r17) + r20
    w[6] = r13 - (a1415 + a1617) - (r18 + r18)
    w[7] = r18 - (r19 + r20)
    w[8] = -((r8 + r9) + (r10 + r12) + (a1113 + r19))
    return w


def react_kernel(planes, u_ref, n_ref, o_ref):
    def block(q, _):
        rows = [pl.ds(pl.multiple_of(8 * planes * q + 8 * h, 8), 8) for h in range(planes)]
        for row in rows:
            for k in range(9, 13):
                o_ref[k, row, :] = u_ref[k, row, :]
        state = []
        fixed = []
        for row in rows:
            u = [u_ref[k, row, :] for k in range(13)]
            rho = total(u[:9])
            internal = u[12] - 0.5 * (u[9] * u[9] + u[10] * u[10] + u[11] * u[11]) / rho
            counts = n_ref[row, :]
            fixed.append((internal, counts, DT / counts.astype(F32)))
            state.append(tuple(u[k] * IW[k] for k in range(9)))

        def substep(i, state):
            new = []
            for c, (internal, counts, step) in zip(state, fixed):
                s1 = total([c[0], c[1], c[5], c[8]])
                s2 = total([c[2], c[6], c[7]])
                heat = 2.5 * s1 + 3.0 * s2 + 1.5 * (c[3] + c[4])
                bound = total([
                    (-1.5 * W[2]) * c[2], (12.0 * W[3]) * c[3], (1.5 * W[4]) * c[4],
                    (0.25 * W[5]) * c[5], (0.02 * W[6]) * c[6], (-0.45 * W[7]) * c[7],
                ])
                w = rates(c, heat / (internal - bound))
                live = i < counts
                new.append(tuple(jnp.where(live, c[k] + step * w[k], c[k]) for k in range(9)))
            return tuple(new)

        state = lax.fori_loop(0, CMAX, substep, tuple(state))
        for row, c in zip(rows, state):
            for k in range(9):
                o_ref[k, row, :] = c[k] * W[k]
        return 0

    lax.fori_loop(0, u_ref.shape[1] // (8 * planes), block, 0)


def react(third, substeps):
    steps = 4
    size = 128 // steps
    return pl.pallas_call(
        functools.partial(react_kernel, 2),
        out_shape=jax.ShapeDtypeStruct((13, 128, 128), F32),
        grid=(steps,),
        in_specs=[
            pl.BlockSpec((13, size, 128), lambda i: (0, i, 0)),
            pl.BlockSpec((size, 128), lambda i: (i, 0)),
        ],
        out_specs=pl.BlockSpec((13, size, 128), lambda i: (0, i, 0)),
        name="react",
    )(third, substeps)


def on_device(sizes, state, fresh, substeps, shift):
    comps, planes, wy, wz = state.shape
    n_tube = sizes[0]
    last = lax.axis_index("tube") == n_tube - 1

    def shifted(k):
        ahead = lax.ppermute(state[:, :k], "tube", [(i, i - 1) for i in range(1, n_tube)])
        ahead = jnp.where(last, fresh[:, None], ahead)
        return jnp.concatenate([state[:, k:], ahead], axis=1)

    start = lax.switch(shift - 1, [functools.partial(shifted, k) for k in range(1, SMAX + 1)])
    third = advance_flow(start.reshape(comps, planes * wy, wz), fresh, sizes)
    out = react(third, substeps.reshape(planes * wy, wz))
    return out.reshape(comps, planes, wy, wz)


def solution(mesh):
    sizes = tuple(mesh.shape[name] for name in ("tube", "gy", "gz"))
    return jax.shard_map(
        functools.partial(on_device, sizes),
        mesh=mesh,
        in_specs=(P(None, "tube", "gy", "gz"), P(None, "gy", "gz"), P("tube", "gy", "gz"), P()),
        out_specs=P(None, "tube", "gy", "gz"),
        check_vma=False,
    )
```

```python
import functools

import jax
import jax.numpy as jnp
import numpy as np
from jax import lax
from jax.experimental import pallas as pl
from jax.experimental.pallas import tpu as pltpu
from jax.sharding import PartitionSpec as P

SMAX = 12
CMAX = 8
DT = 0.05
W = [float(w) for w in np.array([2.016, 31.998, 18.015, 1.008, 15.999, 17.007, 33.006, 34.014, 28.014]) / 18.015]
IW = [1.0 / w for w in W]
MESH = pl.DeviceIdType.MESH
F32 = jnp.float32


def total(parts):
    while len(parts) > 1:
        parts = [a + b for a, b in zip(parts[::2], parts[1::2])] + ([parts[-1]] if len(parts) % 2 else [])
    return parts[0]


def gas(u):
    rho = total(list(u[:9]))
    c = [u[k] * IW[k] for k in range(9)]
    s1 = total([c[0], c[1], c[5], c[8]])
    s2 = total([c[2], c[6], c[7]])
    s3 = c[3] + c[4]
    gas_sum = s1 + s2 + s3
    heat = 2.5 * s1 + 3.0 * s2 + 1.5 * s3
    bound = total([-1.5 * u[2], 12.0 * u[3], 1.5 * u[4], 0.25 * u[5], 0.02 * u[6], -0.45 * u[7]])
    r = 1.0 / rho
    kinetic = 0.5 * r * (u[9] * u[9] + u[10] * u[10] + u[11] * u[11])
    over = 1.0 / heat
    pressure = gas_sum * ((u[12] - kinetic - bound) * over)
    sound = jnp.sqrt((1.0 + gas_sum * over) * pressure * r)
    return r, pressure, sound


def one_side(e1, e2, e3, e4):
    k2 = e2 * e2 * 0.609375 + 3e-6
    k3 = e3 * e3 * 0.609375 + 3e-6
    ta = e1 - 1.375 * e2
    tb = e3 - 0.625 * e2
    tc = e4 - 1.375 * e3
    ra = 1.0 / (ta * ta + k2)
    rb = 1.0 / (tb * tb + k2)
    rc = 1.0 / (tc * tc + k3)
    d23 = e3 - e2
    a = ta + tb
    c = d23 - (e4 - e3)
    wa = ra * ra
    wb = rb * rb * 6.0
    wc = rc * rc * 3.0
    return (wc * c - wa * (a + a)) / (wa + wb + wc) - d23


def face(pair_sum, alpha, df, du):
    p = [alpha * d for d in du]
    plus = [df[k] + p[k] for k in range(4)]
    minus = [df[k] - p[k] for k in range(1, 5)]
    x = one_side(plus[0], plus[1], plus[2], plus[3])
    y = one_side(minus[3], minus[2], minus[1], minus[0])
    return 6.0 * pair_sum + (x - y)


def sweep(lo, hi, value, speed, extra, kind, alpha, emit, before=None, after=None):
    us, fs, du, df = {}, {}, {}, {}

    def cell(i):
        u = value(i)
        v = speed(i)
        if kind == 0:
            f = u * v
        elif kind == 1:
            f = u * v + extra(i)
        else:
            f = (u + extra(i)) * v
        us[i], fs[i] = u, f

    def diff(i):
        cell(i + 1)
        du[i] = us[i + 1] - us[i]
        df[i] = fs[i + 1] - fs[i]

    cell(lo - 2)
    for i in range(lo - 2, lo + 2):
        diff(i)
    head = None
    for j in range(lo, hi + 1):
        diff(j + 2)
        now = face(
            fs[j] + fs[j + 1],
            alpha(j),
            [df[j + k] for k in range(-2, 3)],
            [du[j + k] for k in range(-2, 3)],
        )
        head = now if head is None else head
        if before is not None:
            emit(j, now - before)
        before = now
    if after is not None:
        emit(hi + 1, after - before)
    return head, before


def widest(m):
    return jnp.maximum(jnp.maximum(jnp.maximum(m[0], m[1]), jnp.maximum(m[2], m[3])), jnp.maximum(m[4], m[5]))


def step_kernel(
    sizes,
    start, fresh, third,
    first, second, acc, accy, accz, turned, ends,
    xlo, xhi, ylo, yhi, ysl, ysh, zu,
    nat, xt, yt, zt, ax, ay, az,
    send, recv,
):
    n_tube, n_gy, n_gz = sizes
    me_t, me_y, me_z = lax.axis_index("tube"), lax.axis_index("gy"), lax.axis_index("gz")
    has_lo, has_hi = me_t > 0, me_t < n_tube - 1
    y_next, y_prev = lax.rem(me_y + 1, n_gy), lax.rem(me_y + n_gy - 1, n_gy)
    z_next, z_prev = lax.rem(me_z + 1, n_gz), lax.rem(me_z + n_gz - 1, n_gz)

    def to(tube=None, gy=None, gz=None):
        return (
            me_t if tube is None else tube,
            me_y if gy is None else gy,
            me_z if gz is None else gz,
        )

    barrier = pltpu.get_barrier_semaphore()
    for there in (to(gy=y_next), to(gy=y_prev), to(gz=z_next), to(gz=z_prev)):
        pl.semaphore_signal(barrier, inc=1, device_id=there, device_id_type=MESH)

    @pl.when(has_lo)
    def _():
        pl.semaphore_signal(barrier, inc=1, device_id=to(tube=me_t - 1), device_id_type=MESH)

    @pl.when(has_hi)
    def _():
        pl.semaphore_signal(barrier, inc=1, device_id=to(tube=me_t + 1), device_id_type=MESH)

    pl.semaphore_wait(barrier, 4 + lax.min(me_t, 1) + lax.min(n_tube - 1 - me_t, 1))

    def remote(src, dst, stage, slot, there):
        return pltpu.make_async_remote_copy(
            src_ref=src, dst_ref=dst, send_sem=send.at[stage, slot], recv_sem=recv.at[stage, slot],
            device_id=there, device_id_type=MESH,
        )

    def copies(stage, cur):
        x_up = remote(cur.at[:, pl.ds(0, 24), :], xhi.at[stage], stage, 0, to(tube=me_t - 1))
        x_down = remote(cur.at[:, pl.ds(104, 24), :], xlo.at[stage], stage, 1, to(tube=me_t + 1))
        y_up = remote(ysh.at[stage], ylo.at[stage], stage, 2, to(gy=y_next))
        y_down = remote(ysl.at[stage], yhi.at[stage], stage, 3, to(gy=y_prev))
        z_up = remote(
            zu.at[stage, :, pl.ds(128, 8), :], zu.at[stage, :, pl.ds(0, 8), :], stage, 4, to(gz=z_next)
        )
        z_down = remote(
            zu.at[stage, :, pl.ds(8, 8), :], zu.at[stage, :, pl.ds(136, 8), :], stage, 5, to(gz=z_prev)
        )
        return x_up, x_down, y_up, y_down, z_up, z_down

    def pack(stage, cur, c):
        zu[stage, c, pl.ds(8, 128), :] = jnp.transpose(cur[c])
        for k in range(3):
            for g in range(2):
                ysl[stage, c, 2 * k + g] = cur[c, pl.ds(64 * g + k, 8, stride=8), :]
                ysh[stage, c, 2 * k + g] = cur[c, pl.ds(64 * g + 5 + k, 8, stride=8), :]

    def launch(stage, cur, c):
        low, high = pl.ds(8, 8), pl.ds(128, 8)
        remote(zu.at[stage, c, high, :], zu.at[stage, c, pl.ds(0, 8), :], stage, 4, to(gz=z_next)).start()
        remote(zu.at[stage, c, low, :], zu.at[stage, c, pl.ds(136, 8), :], stage, 5, to(gz=z_prev)).start()

        @pl.when(has_lo)
        def _():
            remote(cur.at[c, pl.ds(0, 24), :], xhi.at[stage, c], stage, 0, to(tube=me_t - 1)).start()

        @pl.when(has_hi)
        def _():
            remote(cur.at[c, pl.ds(104, 24), :], xlo.at[stage, c], stage, 1, to(tube=me_t + 1)).start()

    def launch_rows(stage):
        remote(ysh.at[stage], ylo.at[stage], stage, 2, to(gy=y_next)).start()
        remote(ysl.at[stage], yhi.at[stage], stage, 3, to(gy=y_prev)).start()

    def regular(d, body):
        @pl.loop(0, 11)
        def _(k):
            body(k + (k + 7 - d) // 16, 0)

        body(9 + d, 1)
        body(12, 2)

    def stage_step(stage, cur, out, a, b):
        x_up, x_down, y_up, y_down, z_up, z_down = copies(stage, cur)

        @pl.loop(0, 8)
        def _(q):
            for h in range(2):
                rows = pl.ds(pl.multiple_of(16 * q + 8 * h, 8), 8)
                u = [cur[c, rows, :] for c in range(13)]
                r, pressure, sound = gas(u)
                nat[0, rows, :] = pressure
                for d in range(3):
                    v = u[9 + d] * r
                    nat[1 + d, rows, :] = v
                    nat[4 + d, rows, :] = jnp.abs(v) + sound

        zt[0, pl.ds(8, 128), :] = jnp.transpose(nat[0])
        zt[1, pl.ds(8, 128), :] = jnp.transpose(nat[3])
        zt[2, pl.ds(8, 128), :] = jnp.transpose(nat[6])

        def x_value(c, i):
            if i < 0:
                return xlo[stage, c, pl.ds(8 * (i + 3), 8), :]
            if i > 15:
                return xhi[stage, c, pl.ds(8 * (i - 16), 8), :]
            return cur[c, pl.ds(8 * i, 8), :]

        def x_of(row, nat_row, i):
            if i < 0:
                return xt[row, i + 3]
            if i > 15:
                return xt[row, i - 13]
            return nat[nat_row, pl.ds(8 * i, 8), :]

        def x_alpha(j):
            ax[j + 1] = widest([x_of(2, 4, j + k) for k in range(-2, 4)])

        def x_sweep(c, kind, lo, hi, **known):
            def emit(i, change):
                rows = pl.ds(8 * i, 8)
                acc[c, rows, :] = change

            return sweep(
                lo, hi, lambda i: x_value(c, i), lambda i: x_of(1, 1, i), lambda i: x_of(0, 0, i),
                kind, lambda j: ax[j + 1], emit, **known,
            )

        for j in range(2, 13):
            x_alpha(j)

        def x_inner(c, kind):
            ends[c, 0], ends[c, 1] = x_sweep(c, kind, 2, 12)

        regular(0, x_inner)

        z_up.wait_recv()
        z_down.wait_recv()
        for h in range(2):
            rows = pl.ds(136 * h, 8)
            r, pressure, sound = gas([zu[stage, c, rows, :] for c in range(13)])
            v = zu[stage, 11, rows, :] * r
            zt[0, rows, :] = pressure
            zt[1, rows, :] = v
            zt[2, rows, :] = jnp.abs(v) + sound

        def z_rows(i):
            return pl.ds(8 + i, 8, stride=16)

        for j in range(-1, 16):
            az[j + 1] = widest([zt[2, z_rows(j + k), :] for k in range(-2, 4)])

        def z_body(c, kind):
            def emit(i, change):
                accz[c, pl.ds(i, 8, stride=16), :] = change

            sweep(
                -1, 15, lambda i: zu[stage, c, z_rows(i), :], lambda i: zt[1, z_rows(i), :],
                lambda i: zt[0, z_rows(i), :], kind, lambda j: az[j + 1], emit,
            )

        regular(2, z_body)

        @pl.when(has_lo)
        def _():
            x_down.wait_recv()

        @pl.when(has_hi)
        def _():
            x_up.wait_recv()

        @pl.when(jnp.logical_not(has_lo))
        def _():
            @pl.loop(0, 13)
            def _(c):
                for k in range(3):
                    xlo[stage, c, pl.ds(8 * k, 8), :] = cur[c, pl.ds(0, 8), :]

        @pl.when(jnp.logical_not(has_hi))
        def _():
            @pl.loop(0, 13)
            def _(c):
                for k in range(3):
                    xhi[stage, c, pl.ds(8 * k, 8), :] = fresh[c]

        for i in (-3, -2, -1, 16, 17, 18):
            u = [x_value(c, i) for c in range(13)]
            r, pressure, sound = gas(u)
            v = u[9] * r
            k = i + 3 if i < 0 else i - 13
            xt[0, k] = pressure
            xt[1, k] = v
            xt[2, k] = jnp.abs(v) + sound

        for j in (-1, 0, 1, 13, 14, 15):
            x_alpha(j)

        def x_outer(c, kind):
            x_sweep(c, kind, -1, 1, after=ends[c, 0])
            x_sweep(c, kind, 13, 15, before=ends[c, 1])
            turned[c] = jnp.transpose(accz[c])

        regular(0, x_outer)

        y_up.wait_recv()
        y_down.wait_recv()

        def y_value(c, g, i):
            if i < 0:
                return ylo[stage, c, 2 * (i + 3) + g]
            if i > 7:
                return yhi[stage, c, 2 * (i - 8) + g]
            return cur[c, pl.ds(64 * g + i, 8, stride=8), :]

        for g in range(2):
            for i in range(-3, 11):
                k = 2 * (i + 3) + g
                if 0 <= i < 8:
                    for row, nat_row in ((0, 0), (1, 2), (2, 5)):
                        yt[row, k] = nat[nat_row, pl.ds(64 * g + i, 8, stride=8), :]
                else:
                    u = [y_value(c, g, i) for c in range(13)]
                    r, pressure, sound = gas(u)
                    v = u[10] * r
                    yt[0, k] = pressure
                    yt[1, k] = v
                    yt[2, k] = jnp.abs(v) + sound
            for j in range(-1, 8):
                ay[2 * (j + 1) + g] = widest([yt[2, 2 * (j + k + 3) + g] for k in range(-2, 4)])

        def y_body(c, kind):
            for g in range(2):
                def emit(i, change):
                    accy[c, pl.ds(16 * i + 8 * g, 8), :] = change

                sweep(
                    -1, 7, lambda i: y_value(c, g, i), lambda i: yt[1, 2 * (i + 3) + g],
                    lambda i: yt[0, 2 * (i + 3) + g], kind, lambda j: ay[2 * (j + 1) + g], emit,
                )

        def update(c):
            across = [accy[c, pl.ds(8 * (p // 8) + p % 8, 8, stride=16), :] for p in range(16)]
            change = acc[c] + turned[c] + jnp.concatenate(across, axis=0)
            moved = b * cur[c] - (b * DT / 12.0) * change
            if a != 0.0:
                moved = a * start[c] + moved
            out[c] = moved
            if stage < 2:
                pack(stage + 1, out, c)

        def send_on(c):
            if stage < 2:
                launch(stage + 1, out, c)

        def order(k):
            return k + (k + 6) // 16

        y_body(0, 0)

        @pl.loop(1, 11)
        def _(k):
            if stage < 2:
                @pl.when(k > 1)
                def _():
                    send_on(order(k - 2))

            update(order(k - 1))
            y_body(order(k), 0)

        send_on(9)
        update(11)
        y_body(10, 1)
        send_on(11)
        update(10)
        y_body(12, 2)
        send_on(10)
        update(12)
        send_on(12)
        if stage < 2:
            launch_rows(stage + 1)

    @pl.loop(0, 13)
    def _(c):
        @pl.when(c > 0)
        def _():
            launch(0, start, c - 1)

        pack(0, start, c)

    launch(0, start, 12)
    launch_rows(0)
    stage_step(0, start, first, 0.0, 1.0)
    stage_step(1, first, second, 0.75, 0.25)
    stage_step(2, second, third, 1.0 / 3.0, 2.0 / 3.0)

    for stage, cur in enumerate((start, first, second)):
        x_up, x_down, y_up, y_down, z_up, z_down = copies(stage, cur)
        for copy in (y_up, y_down, z_up, z_down):
            copy.wait_send()

        @pl.when(has_lo)
        def _():
            x_up.wait_send()

        @pl.when(has_hi)
        def _():
            x_down.wait_send()


def advance_flow(start, fresh, sizes):
    tile = (8, 128)
    vmem = pl.BlockSpec(memory_space=pltpu.VMEM)
    scratch = [
        pltpu.VMEM((13, 128, 128), F32),
        pltpu.VMEM((13, 128, 128), F32),
        pltpu.VMEM((13, 128, 128), F32),
        pltpu.VMEM((13, 128, 128), F32),
        pltpu.VMEM((13, 128, 128), F32),
        pltpu.VMEM((13, 128, 128), F32),
        pltpu.VMEM((13, 2) + tile, F32),
        pltpu.VMEM((3, 13, 24, 128), F32),
        pltpu.VMEM((3, 13, 24, 128), F32),
        pltpu.VMEM((3, 13, 6) + tile, F32),
        pltpu.VMEM((3, 13, 6) + tile, F32),
        pltpu.VMEM((3, 13, 6) + tile, F32),
        pltpu.VMEM((3, 13, 6) + tile, F32),
        pltpu.VMEM((3, 13, 144, 128), F32),
        pltpu.VMEM((7, 128, 128), F32),
        pltpu.VMEM((3, 6) + tile, F32),
        pltpu.VMEM((3, 28) + tile, F32),
        pltpu.VMEM((3, 144, 128), F32),
        pltpu.VMEM((17,) + tile, F32),
        pltpu.VMEM((18,) + tile, F32),
        pltpu.VMEM((17,) + tile, F32),
        pltpu.SemaphoreType.DMA((3, 6)),
        pltpu.SemaphoreType.DMA((3, 6)),
    ]
    return pl.pallas_call(
        functools.partial(step_kernel, sizes),
        out_shape=jax.ShapeDtypeStruct((13, 128, 128), F32),
        in_specs=[vmem, vmem],
        out_specs=vmem,
        scratch_shapes=scratch,
        compiler_params=pltpu.CompilerParams(collective_id=0, has_side_effects=True),
        name="flow",
    )(start, fresh)


def rates(c, y):
    h = jnp.exp(-0.5 * y)
    g = jnp.exp(-0.3 * y)
    e1 = h * h
    e15 = e1 * h
    e3 = e15 * e15
    e4 = e3 * e1
    e45 = e3 * e15
    e5 = e4 * e1
    e6 = e3 * e3
    e08 = h * g
    c31 = c[3] * c[1]
    c45 = c[4] * c[5]
    c40 = c[4] * c[0]
    c35 = c[3] * c[5]
    n0 = 30.0 * e4 * c31 - 8.0 * e1 * c45
    n2 = 20.0 * e3 * c40 - 6.0 * e15 * c35
    n4 = 25.0 * e15 * (c[0] * c[5]) - 10.0 * e45 * (c[2] * c[3])
    n6 = 12.0 * e4 * (c[4] * c[2]) - 5.0 * e15 * (c[5] * c[5])
    r8 = 4.0 * e6 * (c[0] * c[8])
    third = h * c[8]
    c34 = c[3] * c[4]
    r9 = 20.0 * third * (c[3] * c[3])
    r10 = 15.0 * third * (c[4] * c[4])
    r11 = 18.0 * third * c34
    r12 = 22.0 * third * c35
    r13 = 25.0 * (g * c[8]) * c31
    c63 = c[6] * c[3]
    r14 = 30.0 * e08 * c63
    r15 = 25.0 * h * c63
    r16 = 20.0 * g * (c[6] * c[4])
    r17 = 30.0 * g * (c[6] * c[5])
    r18 = 10.0 * h * (c[6] * c[6])
    r19 = 6.0 * e5 * (c[7] * c[8])
    r20 = 15.0 * e15 * (c[7] * c[3])
    s89 = r8 - r9
    a1113 = r11 + r13
    a1415 = r14 + r15
    a1617 = r16 + r17
    w = [None] * 9
    w[0] = (r14 - n2) - (n4 + s89)
    w[1] = (r10 - n0) + (r14 - r13) + (a1617 + r18)
    w[2] = (n4 - n6) + (r12 + r17) + r20
    w[3] = (n2 - n0) + (n4 + (s89 + s89)) - (a1113 + r12) - (a1415 + r20)
    w[4] = (n0 - n2) - n6 - (r10 + r10) - (r11 + r16)
    two = n6 + r15 + r19
    w[5] = (n0 + n2) - n4 + (two + two) + (r11 - r12) + (r16 - r17) + r20
    w[6] = r13 - (a1415 + a1617) - (r18 + r18)
    w[7] = r18 - (r19 + r20)
    w[8] = -((r8 + r9) + (r10 + r12) + (a1113 + r19))
    return w


def react_kernel(planes, u_ref, n_ref, o_ref):
    def block(q, _):
        rows = [pl.ds(pl.multiple_of(8 * planes * q + 8 * h, 8), 8) for h in range(planes)]
        for row in rows:
            for k in range(9, 13):
                o_ref[k, row, :] = u_ref[k, row, :]
        state = []
        fixed = []
        for row in rows:
            u = [u_ref[k, row, :] for k in range(13)]
            rho = total(u[:9])
            internal = u[12] - 0.5 * (u[9] * u[9] + u[10] * u[10] + u[11] * u[11]) / rho
            counts = n_ref[row, :]
            fixed.append((internal, counts, DT / counts.astype(F32)))
            state.append(tuple(u[k] * IW[k] for k in range(9)))

        def substep(i, state):
            new = []
            for c, (internal, counts, step) in zip(state, fixed):
                s1 = total([c[0], c[1], c[5], c[8]])
                s2 = total([c[2], c[6], c[7]])
                heat = 2.5 * s1 + 3.0 * s2 + 1.5 * (c[3] + c[4])
                bound = total([
                    (-1.5 * W[2]) * c[2], (12.0 * W[3]) * c[3], (1.5 * W[4]) * c[4],
                    (0.25 * W[5]) * c[5], (0.02 * W[6]) * c[6], (-0.45 * W[7]) * c[7],
                ])
                w = rates(c, heat / (internal - bound))
                live = i < counts
                new.append(tuple(jnp.where(live, c[k] + step * w[k], c[k]) for k in range(9)))
            return tuple(new)

        state = lax.fori_loop(0, CMAX, substep, tuple(state))
        for row, c in zip(rows, state):
            for k in range(9):
                o_ref[k, row, :] = c[k] * W[k]
        return 0

    lax.fori_loop(0, u_ref.shape[1] // (8 * planes), block, 0)


def react(third, substeps):
    steps = 4
    size = 128 // steps
    return pl.pallas_call(
        functools.partial(react_kernel, 2),
        out_shape=jax.ShapeDtypeStruct((13, 128, 128), F32),
        grid=(steps,),
        in_specs=[
            pl.BlockSpec((13, size, 128), lambda i: (0, i, 0)),
            pl.BlockSpec((size, 128), lambda i: (i, 0)),
        ],
        out_specs=pl.BlockSpec((13, size, 128), lambda i: (0, i, 0)),
        name="react",
    )(third, substeps)


def on_device(sizes, state, fresh, substeps, shift):
    comps, planes, wy, wz = state.shape
    n_tube = sizes[0]
    last = lax.axis_index("tube") == n_tube - 1

    def shifted(k):
        ahead = lax.ppermute(state[:, :k], "tube", [(i, i - 1) for i in range(1, n_tube)])
        ahead = jnp.where(last, fresh[:, None], ahead)
        return jnp.concatenate([state[:, k:], ahead], axis=1)

    start = lax.switch(shift - 1, [functools.partial(shifted, k) for k in range(1, SMAX + 1)])
    third = advance_flow(start.reshape(comps, planes * wy, wz), fresh, sizes)
    out = react(third, substeps.reshape(planes * wy, wz))
    return out.reshape(comps, planes, wy, wz)


def solution(mesh):
    sizes = tuple(mesh.shape[name] for name in ("tube", "gy", "gz"))
    return jax.shard_map(
        functools.partial(on_device, sizes),
        mesh=mesh,
        in_specs=(P(None, "tube", "gy", "gz"), P(None, "gy", "gz"), P("tube", "gy", "gz"), P()),
        out_specs=P(None, "tube", "gy", "gz"),
        check_vma=False,
    )
```
